32 devices in a mesh: light: 4 (over z), pix: 4 (over x, core), cam: 2 (over y).
Axes of the slice: x: 2, y: 2, z: 4, core: 2. Of those that a mesh axis runs over, the one named last changes fastest.
Arguments:
- reflectance: bfloat16 [1024, 32, 4096], P('light', 'cam', 'pix'), may hold values from -120 to 120
- start_basis: float32 [1024, 128], replicated, may hold values from -6 to 6
Outputs:
- core_tensor: float32 [128, 32, 4096], P('light', 'cam', 'pix')
- light_basis: float32 [1024, 128], P('light')
The draws below stay inside these ranges and needn't reach their ends.
All inputs are finite; a program needn't handle non-finite values.
Results may differ from the reference program's by a relative error of at most 0.015.
Values may be sent and summed in bfloat16 or wider, within the bound.
A program may use at most 128 MiB of HBM per device.

```python
import math
import jax
import jax.numpy as jnp
from jax import lax

L = 1024
C = 32
R = 128
ITERS = 2
P_SIZE = 4096
L_DEV = 256
N_LIGHT = 4


def draw_reflectance(key, part):
    subkeys = jax.random.split(key, 6)
    noise_part = jnp.clip(jax.random.normal(subkeys[0], (L, C, P_SIZE), jnp.float32), -6.0, 6.0)
    pixel_scale = jnp.exp(jax.random.uniform(subkeys[1], (1, 1, P_SIZE), jnp.float32, math.log(0.3), math.log(3.0)))
    strength = 0.035
    light_scale = jnp.exp(jax.random.uniform(subkeys[2], (L, 1, 1), jnp.float32, 0.0, math.log(3.0)))
    camera_scale = jnp.exp(jax.random.uniform(subkeys[3], (1, C, 1), jnp.float32, math.log(0.5), math.log(2.0)))
    loadings = jnp.clip(jax.random.normal(subkeys[4], (4, L), jnp.float32), -4.0, 4.0)
    patterns = jnp.clip(jax.random.normal(subkeys[5], (4, C, P_SIZE), jnp.float32), -4.0, 4.0)
    blended = noise_part
    for factor in range(4):
        blended = blended + strength * loadings[factor][:, None, None] * patterns[factor][None, :, :]
    scaled = blended * light_scale * camera_scale * pixel_scale
    return jnp.clip(scaled, -120.0, 120.0).astype(jnp.bfloat16)


def noise(rng, extent, scale, reach, kind=jnp.bfloat16):
    array = scale * jax.random.normal(rng, extent, jnp.float32)
    return jnp.clip(array, min=-reach, max=reach).astype(kind)


def setup_inputs(seed: int = 0) -> dict:
    arg_keys = jax.random.split(jax.random.key(seed), 3)
    reflectance = draw_reflectance(jax.random.fold_in(arg_keys[2], 71), 0)
    start_basis = noise(arg_keys[1], (L, R), 1.0, 6.0, jnp.float32)
    return dict(reflectance=reflectance, start_basis=start_basis)


def orthonormal(image_full):
    inner_gram = jnp.dot(image_full.T.astype(jnp.float32), image_full.astype(jnp.float32), preferred_element_type=jnp.float32, precision=lax.Precision.HIGHEST)
    factor = jnp.linalg.cholesky(inner_gram)
    return lax.linalg.triangular_solve(factor, image_full, left_side=False, lower=True, transpose_a=True)

def reference(reflectance, start_basis):
    fibers = reflectance.reshape(L, C * P_SIZE).astype(jnp.float32)
    gram = jnp.dot(fibers.astype(jnp.float32), fibers.T.astype(jnp.float32), preferred_element_type=jnp.float32) * (1.0 / (C * P_SIZE))
    basis_now = start_basis
    for iteration in range(ITERS):
        image_full = jnp.dot(gram.astype(jnp.float32), basis_now.astype(jnp.float32), preferred_element_type=jnp.float32, precision=lax.Precision.HIGHEST)
        basis_now = orthonormal(image_full)
    rounded = basis_now.astype(jnp.bfloat16)
    light_blocks = reflectance.reshape(N_LIGHT, L_DEV, C * P_SIZE)
    basis_blocks = rounded.reshape(N_LIGHT, L_DEV, R)

    def add_block(running, paired):
        block_rows, block_basis = paired
        product = jnp.dot(block_basis.astype(jnp.float32).T.astype(jnp.float32), block_rows.astype(jnp.float32), preferred_element_type=jnp.float32)
        narrowed = lax.optimization_barrier(product.astype(jnp.bfloat16))
        return (running + narrowed.astype(jnp.float32), None)
    core_flat, unused = lax.scan(add_block, jnp.zeros((R, C * P_SIZE), jnp.float32), (light_blocks, basis_blocks))
    return (core_flat.reshape(R, C, P_SIZE), basis_now)
```

```python
import functools

import jax
import jax.numpy as jnp
from jax import lax
from jax.experimental import pallas as pl
from jax.experimental.pallas import tpu as pltpu
from jax.sharding import PartitionSpec as P

ITERS = 2
MESH = pl.DeviceIdType.MESH


def greet(barrier, devices):
    for device in devices:
        pl.semaphore_signal(barrier, inc=1, device_id=device, device_id_type=MESH)
    pl.semaphore_wait(barrier, len(devices))


def triangular_inverse(inner):
    rank = inner.shape[0]
    height = 8
    shape = (height, rank)
    sub = lax.broadcasted_iota(jnp.int32, shape, 0)
    lane = lax.broadcasted_iota(jnp.int32, shape, 1)
    count = rank // height
    left = [inner[height * t : height * (t + 1), :] for t in range(count)]
    right = [jnp.where(lane == sub + height * t, 1.0, 0.0) for t in range(count)]

    def spread_row(tile, k):
        return jnp.broadcast_to(tile[k : k + 1, :], shape)

    def spread_column(tile, j):
        return jnp.broadcast_to(tile[:, j : j + 1], shape)

    for p in range(count):
        first = height * p
        top, below = left[p], right[p]
        columns = [spread_column(top, first + k) for k in range(height)]
        inverses, pivots = [], jnp.ones(shape, jnp.float32)
        for k in range(height):
            pivot = spread_row(columns[k], k)
            inverse = 1.0 / pivot
            pivots = jnp.where(sub == k, pivot, pivots)
            inverses.append(inverse)
            factor = jnp.where(sub > k, columns[k] * inverse, 0.0)
            for later in range(k + 1, height):
                columns[later] = columns[later] - factor * spread_row(columns[later], k)
            top = top - factor * spread_row(top, k)
            below = below - factor * spread_row(below, k)
        right[p] = below * lax.rsqrt(pivots)
        top_rows = [spread_row(top, k) * inverses[k] for k in range(height)]
        below_rows = [spread_row(below, k) * inverses[k] for k in range(height)]
        steps = [
            [spread_row(columns[later], k) * inverses[k] for later in range(k + 1, height)]
            for k in range(height)
        ]
        for t in range(p + 1, count):
            own = [spread_column(left[t], first + k) for k in range(height)]
            upper, lower = left[t], right[t]
            for k in range(height):
                for index, later in enumerate(range(k + 1, height)):
                    own[later] = own[later] - own[k] * steps[k][index]
                upper = upper - own[k] * top_rows[k]
                lower = lower - own[k] * below_rows[k]
            left[t], right[t] = upper, lower
    return jnp.concatenate(right, axis=0)


def orthonormal(image):
    inner = lax.dot_general(image, image, (((0,), (0,)), ((), ())), preferred_element_type=jnp.float32)
    inverse = triangular_inverse(inner)
    pieces = []
    for _ in range(3):
        piece = inverse.astype(jnp.bfloat16)
        pieces.append(piece)
        inverse = inverse - piece.astype(jnp.float32)
    basis = None
    for piece in reversed(pieces):
        term = lax.dot_general(image, piece, (((1,), (1,)), ((), ())), preferred_element_type=jnp.float32)
        basis = term if basis is None else basis + term
    return basis


def step_kernel(lights, pixes, cams, blocks, subs, scale, source_ref, start_ref, core_ref, rows_ref,
                arrived, turned, every, left, total, gram, gram16, whole, basis16,
                part, plane_buf, own_buf, light_buf, image, ysend, yrecv,
                load_sem, own_sem, start_sem, first_send, first_recv, chunk_send, chunk_recv,
                send1, recv1, send2, recv2, send3, recv3, send4, recv4):
    light = lax.axis_index("light")
    plane = pixes * cams
    me = lax.axis_index("pix") * cams + lax.axis_index("cam")
    rows, own_cams, width = source_ref.shape
    parts = own_cams // lights
    pieces, chunks, piece = turned.shape[1], every.shape[0], every.shape[2]
    rank = rows_ref.shape[1]
    height = rows // blocks
    peers = [lax.rem(light + step, lights) for step in range(1, lights)]
    light_devices = [{"light": peer} for peer in peers]
    plane_peers = [lax.rem(me + step, plane) for step in range(1, plane)]
    plane_devices = [{"pix": peer // cams, "cam": lax.rem(peer, cams)} for peer in plane_peers]

    def load(block):
        return pltpu.make_async_copy(
            source_ref.at[pl.ds(block * height, height)], arrived.at[block % 2], load_sem.at[block % 2]
        )

    load(0).start()
    load_start = pltpu.make_async_copy(start_ref, whole, start_sem)
    load_start.start()
    greet(pltpu.get_barrier_semaphore(), plane_devices + light_devices)

    def own_rows(start, size):
        return pl.ds(pl.multiple_of(light * rows + start, 16), size)

    def first_copy(slot, block):
        return pltpu.make_async_remote_copy(
            src_ref=turned.at[peers[slot] * parts, :, pl.ds(block * height, height)],
            dst_ref=every.at[pl.ds(0, pieces), own_rows(block * height, height)],
            send_sem=first_send.at[slot, block],
            recv_sem=first_recv.at[slot, block],
            device_id=light_devices[slot],
            device_id_type=MESH,
        )

    def chunk_copy(slot, chunk):
        return pltpu.make_async_remote_copy(
            src_ref=turned.at[peers[slot] * parts + chunk // pieces, lax.rem(chunk, pieces)],
            dst_ref=every.at[chunk, own_rows(0, rows)],
            send_sem=chunk_send.at[slot, chunk - pieces],
            recv_sem=chunk_recv.at[slot, chunk - pieces],
            device_id=light_devices[slot],
            device_id_type=MESH,
        )

    def own_copy(part_index):
        return pltpu.make_async_copy(
            turned.at[light * parts + part_index],
            every.at[pl.ds(part_index * pieces, pieces), own_rows(0, rows)],
            own_sem.at[part_index],
        )

    step_rows = 16
    for block in range(blocks):
        if block + 1 < blocks:
            load(block + 1).start()
        load(block).wait()

        def turn(index, carry):
            start = pl.multiple_of(index * step_rows, step_rows)
            some = jnp.transpose(arrived[block % 2, pl.ds(start, step_rows)], (1, 0, 2))
            spot = pl.ds(pl.multiple_of(block * height + start, step_rows), step_rows)
            for q in range(pieces):
                turned[:, q, spot, :] = some[:, :, q * piece : (q + 1) * piece]
            return carry

        lax.fori_loop(0, height // step_rows, turn, 0)
        for slot in range(lights - 1):
            first_copy(slot, block).start()
    for chunk in range(pieces, chunks):
        for slot in range(lights - 1):
            chunk_copy(slot, chunk).start()
    for index in range(parts):
        own_copy(index).start()

    load_start.wait()
    basis = whole[...]
    high = basis.astype(jnp.bfloat16)
    left[:rank] = high.T
    left[rank:] = (basis - high.astype(jnp.float32)).astype(jnp.bfloat16).T
    total[...] = jnp.zeros_like(total)
    gram[...] = jnp.zeros_like(gram)
    for index in range(parts):
        own_copy(index).wait()

    def project(chunk):
        some = every[chunk]
        halves = jnp.dot(left[...], some, preferred_element_type=jnp.float32)
        projected = (halves[:rank] + halves[rank:]).astype(jnp.bfloat16)
        total[...] += lax.dot_general(
            some, projected, (((1,), (1,)), ((), ())), preferred_element_type=jnp.float32
        )

    def correlate(chunk):
        for index in range(lights):
            spot = pl.ds(index * rows, rows)
            gram[spot, :] += lax.dot_general(
                every[chunk, spot], every[chunk], (((1,), (1,)), ((), ())), preferred_element_type=jnp.float32
            )

    for slot in range(lights - 1):
        for block in range(blocks):
            first_copy(slot, block).wait_recv()

    def both(chunk, carry):
        project(chunk)
        correlate(chunk)
        return carry

    def later(chunk, carry):
        for slot in range(lights - 1):
            chunk_copy(slot, chunk).wait_recv()
        return both(chunk, carry)

    last = chunks - 1
    if chunks == pieces:
        lax.fori_loop(0, last, both, 0)
    else:
        lax.fori_loop(0, pieces, both, 0)
        lax.fori_loop(pieces, last, later, 0)
        for slot in range(lights - 1):
            chunk_copy(slot, last).wait_recv()
    project(last)

    shard = part.shape[1] // plane
    sub_rows = shard // subs

    def shard_rows(index, sub):
        return pl.ds(pl.multiple_of(index * shard + sub * sub_rows, sub_rows), sub_rows)

    def all_reduce(it, meanwhile):
        def copy1(slot, sub):
            return pltpu.make_async_remote_copy(
                src_ref=part.at[it, shard_rows(plane_peers[slot], sub)],
                dst_ref=plane_buf.at[it, slot, sub],
                send_sem=send1.at[it, slot, sub],
                recv_sem=recv1.at[it, slot, sub],
                device_id=plane_devices[slot],
                device_id_type=MESH,
            )

        def copy2(slot, sub):
            return pltpu.make_async_remote_copy(
                src_ref=own_buf.at[it, sub],
                dst_ref=light_buf.at[it, light, sub],
                send_sem=send2.at[it, slot, sub],
                recv_sem=recv2.at[it, slot, sub],
                device_id=light_devices[slot],
                device_id_type=MESH,
            )

        def copy3(slot, sub):
            return pltpu.make_async_remote_copy(
                src_ref=image.at[it, shard_rows(me, sub)],
                dst_ref=image.at[it, shard_rows(me, sub)],
                send_sem=send3.at[it, slot, sub],
                recv_sem=recv3.at[it, slot, sub],
                device_id=plane_devices[slot],
                device_id_type=MESH,
            )

        everyone, others = range(plane - 1), range(lights - 1)
        for sub in range(subs):
            for slot in everyone:
                copy1(slot, sub).start()
        meanwhile()
        for sub in range(subs):
            summed = part[it, shard_rows(me, sub), :].astype(jnp.float32)
            for slot in everyone:
                copy1(slot, sub).wait_recv()
                summed += plane_buf[it, slot, sub].astype(jnp.float32)
            own_buf[it, sub] = summed.astype(own_buf.dtype)
            for slot in others:
                copy2(slot, sub).start()
            light_buf[it, light, sub] = summed.astype(own_buf.dtype)
        for sub in range(subs):
            for slot in others:
                copy2(slot, sub).wait_recv()
            summed = light_buf[it, 0, sub].astype(jnp.float32)
            for index in range(1, lights):
                summed += light_buf[it, index, sub].astype(jnp.float32)
            image[it, shard_rows(me, sub), :] = summed.astype(image.dtype)
            for slot in everyone:
                copy3(slot, sub).start()
        for sub in range(subs):
            for slot in everyone:
                copy3(slot, sub).wait_recv()

        def finish():
            for sub in range(subs):
                for slot in everyone:
                    copy1(slot, sub).wait_send()
                    copy3(slot, sub).wait_send()
                for slot in others:
                    copy2(slot, sub).wait_send()

        return finish

    finishes = []
    for it in range(ITERS):
        if it == 0:
            part[it] = (total[...] * scale).astype(part.dtype)

            def meanwhile():
                correlate(last)
                gram16[...] = gram[...].astype(jnp.bfloat16)
        else:
            high = basis.astype(jnp.bfloat16)
            basis16[:, :rank] = high
            basis16[:, rank:] = (basis - high.astype(jnp.float32)).astype(jnp.bfloat16)
            halves = jnp.dot(gram16[...], basis16[...], preferred_element_type=jnp.float32)
            part[it] = ((halves[:, :rank] + halves[:, rank:]) * scale).astype(part.dtype)

            def meanwhile():
                pass
        finishes.append(all_reduce(it, meanwhile))
        basis = orthonormal(image[it])

    basis16[:, :rank] = basis.astype(jnp.bfloat16)
    share = rank // lights

    def copy4(slot, index):
        group = pl.ds(index * pieces, pieces)
        return pltpu.make_async_remote_copy(
            src_ref=ysend.at[peers[slot], group],
            dst_ref=yrecv.at[light, group],
            send_sem=send4.at[slot, index],
            recv_sem=recv4.at[slot, index],
            device_id=light_devices[slot],
            device_id_type=MESH,
        )

    for index in range(parts):
        for q in range(pieces):
            chunk = index * pieces + q
            y = lax.dot_general(
                basis16[:, :rank], every[chunk], (((0,), (0,)), ((), ())), preferred_element_type=jnp.float32
            ).astype(ysend.dtype)
            for k in range(lights):
                ysend[k, chunk] = y[k * share : (k + 1) * share]
        for slot in range(lights - 1):
            copy4(slot, index).start()
        yrecv[light, pl.ds(index * pieces, pieces)] = ysend[light, pl.ds(index * pieces, pieces)]
    whole[...] = basis
    rows_ref[...] = whole[own_rows(0, rows), :]
    for finish in finishes:
        finish()
    for slot in range(lights - 1):
        for block in range(blocks):
            first_copy(slot, block).wait_send()
        for chunk in range(pieces, chunks):
            chunk_copy(slot, chunk).wait_send()
    for index in range(parts):
        for slot in range(lights - 1):
            copy4(slot, index).wait_recv()
        for k in range(lights):
            for q in range(pieces):
                core_ref[:, k * parts + index, q * piece : (q + 1) * piece] = yrecv[k, index * pieces + q].astype(
                    core_ref.dtype
                )
    for index in range(parts):
        for slot in range(lights - 1):
            copy4(slot, index).wait_send()


def per_device(reflectance, start_basis):
    rows, own_cams, width = reflectance.shape
    rank = start_basis.shape[1]
    lights, pixes, cams = (lax.axis_size(name) for name in ("light", "pix", "cam"))
    plane = pixes * cams
    all_rows, share, parts = rows * lights, rank // lights, own_cams // lights
    scale = 1.0 / (own_cams * width * cams * pixes)
    piece = min(256, width)
    pieces = width // piece
    chunks = parts * pieces
    blocks = max(1, rows // 32)
    shard = all_rows // plane
    subs = 2
    vmem, anywhere = pl.BlockSpec(memory_space=pltpu.VMEM), pl.BlockSpec(memory_space=pl.ANY)
    dma = pltpu.SemaphoreType.DMA
    bf16, f32 = jnp.bfloat16, jnp.float32
    sub_shape = (subs, shard // subs, rank)
    return pl.pallas_call(
        functools.partial(step_kernel, lights, pixes, cams, blocks, subs, scale),
        out_shape=(
            jax.ShapeDtypeStruct((share, own_cams, width), f32),
            jax.ShapeDtypeStruct((rows, rank), f32),
        ),
        in_specs=[anywhere, anywhere],
        out_specs=(vmem, vmem),
        scratch_shapes=[
            pltpu.VMEM((2, rows // blocks, own_cams, width), bf16),
            pltpu.VMEM((own_cams, pieces, rows, piece), bf16),
            pltpu.VMEM((chunks, all_rows, piece), bf16),
            pltpu.VMEM((2 * rank, all_rows), bf16),
            pltpu.VMEM((all_rows, rank), f32),
            pltpu.VMEM((all_rows, all_rows), f32),
            pltpu.VMEM((all_rows, all_rows), bf16),
            pltpu.VMEM((all_rows, rank), f32),
            pltpu.VMEM((all_rows, 2 * rank), bf16),
            pltpu.VMEM((ITERS, all_rows, rank), bf16),
            pltpu.VMEM((ITERS, plane - 1) + sub_shape, bf16),
            pltpu.VMEM((ITERS,) + sub_shape, bf16),
            pltpu.VMEM((ITERS, lights) + sub_shape, bf16),
            pltpu.VMEM((ITERS, all_rows, rank), bf16),
            pltpu.VMEM((lights, chunks, share, piece), bf16),
            pltpu.VMEM((lights, chunks, share, piece), bf16),
            dma((2,)), dma((parts,)), dma,
            dma((lights - 1, blocks)), dma((lights - 1, blocks)),
            dma((lights - 1, max(1, chunks - pieces))), dma((lights - 1, max(1, chunks - pieces))),
            dma((ITERS, plane - 1, subs)), dma((ITERS, plane - 1, subs)),
            dma((ITERS, lights - 1, subs)), dma((ITERS, lights - 1, subs)),
            dma((ITERS, plane - 1, subs)), dma((ITERS, plane - 1, subs)),
            dma((lights - 1, parts)), dma((lights - 1, parts)),
        ],
        compiler_params=pltpu.CompilerParams(
            collective_id=0, has_side_effects=True, vmem_limit_bytes=60 * 1024 * 1024
        ),
    )(reflectance, start_basis)


def solution(mesh):
    return jax.shard_map(
        per_device,
        mesh=mesh,
        in_specs=(P("light", "cam", "pix"), P()),
        out_specs=(P("light", "cam", "pix"), P("light", None)),
        check_vma=False,
    )
```

```python
import functools

import jax
import jax.numpy as jnp
from jax import lax
from jax.experimental import pallas as pl
from jax.experimental.pallas import tpu as pltpu
from jax.sharding import PartitionSpec as P

ITERS = 2
MESH = pl.DeviceIdType.MESH


def greet(barrier, devices):
    for device in devices:
        pl.semaphore_signal(barrier, inc=1, device_id=device, device_id_type=MESH)
    pl.semaphore_wait(barrier, len(devices))


def offsets(count):
    even = range(0, count, 2)
    return [(turn, swap) for turn in reversed(even) for swap in (1, 0) if turn or swap]


def moved(place, count, offset):
    turn, swap = offset
    there = lax.rem(place + turn, count)
    return there + (1 - 2 * lax.rem(there, 2)) if swap else there


def triangular_inverse(inner):
    rank = inner.shape[0]
    height = 8
    shape = (height, rank)
    sub = lax.broadcasted_iota(jnp.int32, shape, 0)
    lane = lax.broadcasted_iota(jnp.int32, shape, 1)
    count = rank // height
    left = [inner[height * t : height * (t + 1), :] for t in range(count)]
    right = [jnp.where(lane == sub + height * t, 1.0, 0.0) for t in range(count)]

    def spread_row(tile, k):
        return jnp.broadcast_to(tile[k : k + 1, :], shape)

    def spread_column(tile, j):
        return jnp.broadcast_to(tile[:, j : j + 1], shape)

    for p in range(count):
        first = height * p
        top, below = left[p], right[p]
        columns = [spread_column(top, first + k) for k in range(height)]
        inverses, pivots = [], jnp.ones(shape, jnp.float32)
        for k in range(height):
            pivot = spread_row(columns[k], k)
            inverse = 1.0 / pivot
            pivots = jnp.where(sub == k, pivot, pivots)
            inverses.append(inverse)
            factor = jnp.where(sub > k, columns[k] * inverse, 0.0)
            for later in range(k + 1, height):
                columns[later] = columns[later] - factor * spread_row(columns[later], k)
            top = top - factor * spread_row(top, k)
            below = below - factor * spread_row(below, k)
        right[p] = below * lax.rsqrt(pivots)
        top_rows = [spread_row(top, k) * inverses[k] for k in range(height)]
        below_rows = [spread_row(below, k) * inverses[k] for k in range(height)]
        steps = [
            [spread_row(columns[later], k) * inverses[k] for later in range(k + 1, height)]
            for k in range(height)
        ]
        for t in range(p + 1, count):
            own = [spread_column(left[t], first + k) for k in range(height)]
            upper, lower = left[t], right[t]
            for k in range(height):
                for index, later in enumerate(range(k + 1, height)):
                    own[later] = own[later] - own[k] * steps[k][index]
                upper = upper - own[k] * top_rows[k]
                lower = lower - own[k] * below_rows[k]
            left[t], right[t] = upper, lower
    return jnp.concatenate(right, axis=0)


def orthonormal(image):
    inner = lax.dot_general(image, image, (((0,), (0,)), ((), ())), preferred_element_type=jnp.float32)
    inverse = triangular_inverse(inner)
    high = inverse.astype(jnp.bfloat16)
    low = (inverse - high.astype(jnp.float32)).astype(jnp.bfloat16)
    return lax.dot_general(
        jnp.concatenate([image, image], axis=1), jnp.concatenate([high, low], axis=1),
        (((1,), (1,)), ((), ())), preferred_element_type=jnp.float32,
    )


def step_kernel(lights, pixes, cams, blocks, subs, scale, source_ref, start_ref, core_ref, rows_ref,
                arrived, turned, every, left, total, gram, gram16, whole, basis16,
                part, plane_buf, own_buf, light_buf, image, ysend, yrecv,
                load_sem, own_sem, start_sem, first_send, first_recv, bulk_send, bulk_recv, chunk_send, chunk_recv,
                send1, recv1, send2, recv2, send3, recv3, send4, recv4):
    light = lax.axis_index("light")
    plane = pixes * cams
    pix, cam = lax.axis_index("pix"), lax.axis_index("cam")
    me = pix * cams + cam
    rows, own_cams, width = source_ref.shape
    parts = own_cams // lights
    pieces, piece = turned.shape[1], every.shape[3]
    others = range(lights - 1)
    rank = rows_ref.shape[1]
    height = rows // blocks
    peers = [moved(light, lights, offset) for offset in offsets(lights)]
    light_devices = [{"light": peer} for peer in peers]
    steps = [(offset, turn) for offset in offsets(pixes) + [(0, 0)] for turn in range(cams) if turn or offset != (0, 0)]
    steps.sort(key=lambda step: -(2 * (step[0][0] > 0) + 2 * (step[1] > 0) + step[0][1]))
    plane_devices = [{"pix": moved(pix, pixes, offset), "cam": lax.rem(cam + turn, cams)} for offset, turn in steps]
    plane_peers = [device["pix"] * cams + device["cam"] for device in plane_devices]

    def load(block):
        return pltpu.make_async_copy(
            source_ref.at[pl.ds(block * height, height)], arrived.at[block % 2], load_sem.at[block % 2]
        )

    load(0).start()
    load_start = pltpu.make_async_copy(start_ref, whole, start_sem)
    load_start.start()
    greet(pltpu.get_barrier_semaphore(), plane_devices + light_devices)

    def own_rows(start, size):
        return pl.ds(pl.multiple_of(light * rows + start, 16), size)

    def first_copy(slot, block):
        return pltpu.make_async_remote_copy(
            src_ref=turned.at[peers[slot] * parts, :, pl.ds(block * height, height)],
            dst_ref=every.at[0, :, own_rows(block * height, height)],
            send_sem=first_send.at[slot, block],
            recv_sem=first_recv.at[slot, block],
            device_id=light_devices[slot],
            device_id_type=MESH,
        )


    def bulk_copy(slot):
        return pltpu.make_async_remote_copy(
            src_ref=turned.at[pl.ds(peers[slot] * parts + 1, parts - 2)],
            dst_ref=every.at[pl.ds(1, parts - 2), :, own_rows(0, rows)],
            send_sem=bulk_send.at[slot],
            recv_sem=bulk_recv.at[slot],
            device_id=light_devices[slot],
            device_id_type=MESH,
        )

    def chunk_copy(slot, q):
        return pltpu.make_async_remote_copy(
            src_ref=turned.at[peers[slot] * parts + parts - 1, q],
            dst_ref=every.at[parts - 1, q, own_rows(0, rows)],
            send_sem=chunk_send.at[slot, q],
            recv_sem=chunk_recv.at[slot, q],
            device_id=light_devices[slot],
            device_id_type=MESH,
        )

    def own_copy(part_index):
        return pltpu.make_async_copy(
            turned.at[light * parts + part_index],
            every.at[part_index, :, own_rows(0, rows)],
            own_sem.at[part_index],
        )

    step_rows = 16
    for block in range(blocks):
        if block + 1 < blocks:
            load(block + 1).start()
        load(block).wait()

        def turn(index, carry):
            start = pl.multiple_of(index * step_rows, step_rows)
            some = jnp.transpose(arrived[block % 2, pl.ds(start, step_rows)], (1, 0, 2))
            spot = pl.ds(pl.multiple_of(block * height + start, step_rows), step_rows)
            for q in range(pieces):
                turned[:, q, spot, :] = some[:, :, q * piece : (q + 1) * piece]
            return carry

        lax.fori_loop(0, height // step_rows, turn, 0)
        for slot in others:
            first_copy(slot, block).start()
    for slot in others:
        if parts > 2:
            bulk_copy(slot).start()
    for q in range(pieces if parts > 1 else 0):
        for slot in others:
            chunk_copy(slot, q).start()
    for index in range(parts):
        own_copy(index).start()

    load_start.wait()
    basis = whole[...]
    high = basis.astype(jnp.bfloat16)
    left[:rank] = high.T
    left[rank:] = (basis - high.astype(jnp.float32)).astype(jnp.bfloat16).T
    total[...] = jnp.zeros_like(total)
    gram[...] = jnp.zeros_like(gram)
    for index in range(parts):
        own_copy(index).wait()

    def project(index, q):
        some = every[index, q]
        halves = jnp.dot(left[...], some, preferred_element_type=jnp.float32)
        projected = (halves[:rank] + halves[rank:]).astype(jnp.bfloat16)
        total[...] += lax.dot_general(
            some, projected, (((1,), (1,)), ((), ())), preferred_element_type=jnp.float32
        )

    def correlate(index, q):
        for block in range(lights):
            spot = pl.ds(block * rows, rows)
            gram[spot, :] += lax.dot_general(
                every[index, q, spot], every[index, q], (((1,), (1,)), ((), ())), preferred_element_type=jnp.float32
            )

    def both(chunk, carry):
        index, q = chunk // pieces, lax.rem(chunk, pieces)
        project(index, q)
        correlate(index, q)
        return carry

    last = parts * pieces - 1
    for slot in others:
        for block in range(blocks):
            first_copy(slot, block).wait_recv()
    lax.fori_loop(0, min(pieces, last), both, 0)
    if parts > 2:
        for slot in others:
            bulk_copy(slot).wait_recv()
        lax.fori_loop(pieces, (parts - 1) * pieces, both, 0)
    for q in range(pieces if parts > 1 else 0):
        for slot in others:
            chunk_copy(slot, q).wait_recv()
        if q < pieces - 1:
            both((parts - 1) * pieces + q, 0)
    project(parts - 1, pieces - 1)

    shard = part.shape[1] // plane
    sub_rows = shard // subs

    def shard_rows(index, sub):
        return pl.ds(pl.multiple_of(index * shard + sub * sub_rows, sub_rows), sub_rows)

    def all_reduce(it, meanwhile):
        def copy1(slot, sub):
            return pltpu.make_async_remote_copy(
                src_ref=part.at[it, shard_rows(plane_peers[slot], sub)],
                dst_ref=plane_buf.at[it, slot, sub],
                send_sem=send1.at[it, slot, sub],
                recv_sem=recv1.at[it, slot, sub],
                device_id=plane_devices[slot],
                device_id_type=MESH,
            )

        def copy2(slot, sub):
            return pltpu.make_async_remote_copy(
                src_ref=own_buf.at[it, sub],
                dst_ref=light_buf.at[it, light, sub],
                send_sem=send2.at[it, slot, sub],
                recv_sem=recv2.at[it, slot, sub],
                device_id=light_devices[slot],
                device_id_type=MESH,
            )

        def copy3(slot, sub):
            return pltpu.make_async_remote_copy(
                src_ref=image.at[it, shard_rows(me, sub)],
                dst_ref=image.at[it, shard_rows(me, sub)],
                send_sem=send3.at[it, slot, sub],
                recv_sem=recv3.at[it, slot, sub],
                device_id=plane_devices[slot],
                device_id_type=MESH,
            )

        everyone = range(plane - 1)
        for sub in range(subs):
            for slot in everyone:
                copy1(slot, sub).start()
        meanwhile()
        for sub in range(subs):
            summed = part[it, shard_rows(me, sub), :].astype(jnp.float32)
            for slot in everyone:
                copy1(slot, sub).wait_recv()
                summed += plane_buf[it, slot, sub].astype(jnp.float32)
            own_buf[it, sub] = summed.astype(own_buf.dtype)
            for slot in others:
                copy2(slot, sub).start()
            light_buf[it, light, sub] = summed.astype(own_buf.dtype)
        for sub in range(subs):
            for slot in others:
                copy2(slot, sub).wait_recv()
            summed = light_buf[it, 0, sub].astype(jnp.float32)
            for index in range(1, lights):
                summed += light_buf[it, index, sub].astype(jnp.float32)
            image[it, shard_rows(me, sub), :] = summed.astype(image.dtype)
            for slot in everyone:
                copy3(slot, sub).start()
        for sub in range(subs):
            for slot in everyone:
                copy3(slot, sub).wait_recv()

        def finish():
            for sub in range(subs):
                for slot in everyone:
                    copy1(slot, sub).wait_send()
                    copy3(slot, sub).wait_send()
                for slot in others:
                    copy2(slot, sub).wait_send()

        return finish

    finishes = []
    for it in range(ITERS):
        if it == 0:
            part[it] = (total[...] * scale).astype(part.dtype)

            def meanwhile():
                correlate(parts - 1, pieces - 1)
                gram16[...] = gram[...].astype(jnp.bfloat16)
        else:
            high = basis.astype(jnp.bfloat16)
            basis16[:, :rank] = high
            basis16[:, rank:] = (basis - high.astype(jnp.float32)).astype(jnp.bfloat16)
            halves = jnp.dot(gram16[...], basis16[...], preferred_element_type=jnp.float32)
            part[it] = ((halves[:, :rank] + halves[:, rank:]) * scale).astype(part.dtype)

            def meanwhile():
                pass
        finishes.append(all_reduce(it, meanwhile))
        basis = orthonormal(image[it])

    basis16[:, :rank] = basis.astype(jnp.bfloat16)
    share = rank // lights

    def copy4(slot, index):
        return pltpu.make_async_remote_copy(
            src_ref=ysend.at[peers[slot], index],
            dst_ref=yrecv.at[light, index],
            send_sem=send4.at[slot, index],
            recv_sem=recv4.at[slot, index],
            device_id=light_devices[slot],
            device_id_type=MESH,
        )

    for index in range(parts):
        for q in range(pieces):
            y = lax.dot_general(
                basis16[:, :rank], every[index, q], (((0,), (0,)), ((), ())), preferred_element_type=jnp.float32
            ).astype(ysend.dtype)
            for k in range(lights):
                ysend[k, index, q] = y[k * share : (k + 1) * share]
        for slot in others:
            copy4(slot, index).start()
        yrecv[light, index] = ysend[light, index]
    whole[...] = basis
    rows_ref[...] = whole[own_rows(0, rows), :]
    for finish in finishes:
        finish()
    for slot in others:
        for block in range(blocks):
            first_copy(slot, block).wait_send()
        if parts > 2:
            bulk_copy(slot).wait_send()
        for q in range(pieces if parts > 1 else 0):
            chunk_copy(slot, q).wait_send()
    for index in range(parts):
        for slot in others:
            copy4(slot, index).wait_recv()
        for k in range(lights):
            for q in range(pieces):
                core_ref[:, k * parts + index, q * piece : (q + 1) * piece] = yrecv[k, index, q].astype(
                    core_ref.dtype
                )
    for index in range(parts):
        for slot in others:
            copy4(slot, index).wait_send()


def per_device(reflectance, start_basis):
    rows, own_cams, width = reflectance.shape
    rank = start_basis.shape[1]
    lights, pixes, cams = (lax.axis_size(name) for name in ("light", "pix", "cam"))
    plane = pixes * cams
    all_rows, share, parts = rows * lights, rank // lights, own_cams // lights
    scale = 1.0 / (own_cams * width * cams * pixes)
    piece = min(256, width)
    pieces = width // piece
    blocks = max(1, rows // 64)
    shard = all_rows // plane
    subs = 2
    vmem, hbm = pl.BlockSpec(memory_space=pltpu.VMEM), pl.BlockSpec(memory_space=pltpu.HBM)
    dma = pltpu.SemaphoreType.DMA
    bf16, f32 = jnp.bfloat16, jnp.float32
    sub_shape = (subs, shard // subs, rank)
    return pl.pallas_call(
        functools.partial(step_kernel, lights, pixes, cams, blocks, subs, scale),
        out_shape=(
            jax.ShapeDtypeStruct((share, own_cams, width), f32),
            jax.ShapeDtypeStruct((rows, rank), f32),
        ),
        in_specs=[hbm, hbm],
        out_specs=(vmem, vmem),
        scratch_shapes=[
            pltpu.VMEM((2, rows // blocks, own_cams, width), bf16),
            pltpu.VMEM((own_cams, pieces, rows, piece), bf16),
            pltpu.VMEM((parts, pieces, all_rows, piece), bf16),
            pltpu.VMEM((2 * rank, all_rows), bf16),
            pltpu.VMEM((all_rows, rank), f32),
            pltpu.VMEM((all_rows, all_rows), f32),
            pltpu.VMEM((all_rows, all_rows), bf16),
            pltpu.VMEM((all_rows, rank), f32),
            pltpu.VMEM((all_rows, 2 * rank), bf16),
            pltpu.VMEM((ITERS, all_rows, rank), bf16),
            pltpu.VMEM((ITERS, plane - 1) + sub_shape, bf16),
            pltpu.VMEM((ITERS,) + sub_shape, bf16),
            pltpu.VMEM((ITERS, lights) + sub_shape, bf16),
            pltpu.VMEM((ITERS, all_rows, rank), bf16),
            pltpu.VMEM((lights, parts, pieces, share, piece), bf16),
            pltpu.VMEM((lights, parts, pieces, share, piece), bf16),
            dma((2,)), dma((parts,)), dma,
            dma((lights - 1, blocks)), dma((lights - 1, blocks)),
            dma((lights - 1,)), dma((lights - 1,)), dma((lights - 1, pieces)), dma((lights - 1, pieces)),
            dma((ITERS, plane - 1, subs)), dma((ITERS, plane - 1, subs)),
            dma((ITERS, lights - 1, subs)), dma((ITERS, lights - 1, subs)),
            dma((ITERS, plane - 1, subs)), dma((ITERS, plane - 1, subs)),
            dma((lights - 1, parts)), dma((lights - 1, parts)),
        ],
        compiler_params=pltpu.CompilerParams(
            collective_id=0, has_side_effects=True, vmem_limit_bytes=44 * 1024 * 1024
        ),
    )(reflectance, start_basis)


def solution(mesh):
    return jax.shard_map(
        per_device,
        mesh=mesh,
        in_specs=(P("light", "cam", "pix"), P()),
        out_specs=(P("light", "cam", "pix"), P("light", None)),
        check_vma=False,
    )
```

```python
import functools

import jax
import jax.numpy as jnp
from jax import lax
from jax.experimental import pallas as pl
from jax.experimental.pallas import tpu as pltpu
from jax.sharding import PartitionSpec as P

ITERS = 2
MESH = pl.DeviceIdType.MESH


def greet(barrier, devices):
    for device in devices:
        pl.semaphore_signal(barrier, inc=1, device_id=device, device_id_type=MESH)
    pl.semaphore_wait(barrier, len(devices))


def offsets(count):
    even = range(0, count, 2)
    return [(turn, swap) for turn in reversed(even) for swap in (1, 0) if turn or swap]


def moved(place, count, offset):
    turn, swap = offset
    there = lax.rem(place + turn, count)
    return there + (1 - 2 * lax.rem(there, 2)) if swap else there


def triangular_inverse(inner):
    rank = inner.shape[0]
    height = 8
    shape = (height, rank)
    sub = lax.broadcasted_iota(jnp.int32, shape, 0)
    lane = lax.broadcasted_iota(jnp.int32, shape, 1)
    count = rank // height
    left = [inner[height * t : height * (t + 1), :] for t in range(count)]
    right = [jnp.where(lane == sub + height * t, 1.0, 0.0) for t in range(count)]

    def spread_row(tile, k):
        return jnp.broadcast_to(tile[k : k + 1, :], shape)

    def spread_column(tile, j):
        return jnp.broadcast_to(tile[:, j : j + 1], shape)

    columns = [spread_column(left[0], k) for k in range(height)]
    for p in range(count):
        first = height * p
        top, below, jordan = left[p], right[p], right[p]
        ahead, own, base = [], [], []
        if p + 1 < count:
            ahead = [spread_column(top, first + height + k) for k in range(height)]
            own = [spread_column(left[p + 1], first + k) for k in range(height)]
            base = [spread_column(left[p + 1], first + height + k) for k in range(height)]
        pivots, inverses = jnp.ones(shape, jnp.float32), jnp.ones(shape, jnp.float32)
        for k in range(height):
            pivot = spread_row(columns[k], k)
            inverse = 1.0 / pivot
            pivots = jnp.where(sub == k, pivot, pivots)
            inverses = jnp.where(sub == k, inverse, inverses)
            factor = columns[k] * inverse
            down = jnp.where(sub > k, factor, 0.0)
            factor = jnp.where(sub != k, factor, 0.0)
            for later in range(k + 1, height):
                columns[later] = columns[later] - factor * spread_row(columns[later], k)
            ahead = [column - factor * spread_row(column, k) for column in ahead]
            top = top - factor * spread_row(top, k)
            jordan = jordan - factor * spread_row(jordan, k)
            below = below - down * spread_row(below, k)
        right[p] = below * lax.rsqrt(pivots)
        if p + 1 == count:
            break
        top, jordan = top * inverses, jordan * inverses
        columns = []
        for k in range(height):
            scaled, column = ahead[k] * inverses, base[k]
            for j in range(height):
                column = column - own[j] * spread_row(scaled, j)
            columns.append(column)
        top_rows = [spread_row(top, k) for k in range(height)]
        below_rows = [spread_row(jordan, k) for k in range(height)]
        for t in range(p + 1, count):
            side = own if t == p + 1 else [spread_column(left[t], first + k) for k in range(height)]
            upper, lower = left[t], right[t]
            for k in range(height):
                upper = upper - side[k] * top_rows[k]
                lower = lower - side[k] * below_rows[k]
            left[t], right[t] = upper, lower
    return jnp.concatenate(right, axis=0)


def orthonormal(image):
    inner = lax.dot_general(image, image, (((0,), (0,)), ((), ())), preferred_element_type=jnp.float32)
    inverse = triangular_inverse(inner)
    high = inverse.astype(jnp.bfloat16)
    low = (inverse - high.astype(jnp.float32)).astype(jnp.bfloat16)
    return lax.dot_general(
        jnp.concatenate([image, image], axis=1), jnp.concatenate([high, low], axis=1),
        (((1,), (1,)), ((), ())), preferred_element_type=jnp.float32,
    )


def step_kernel(lights, pixes, cams, blocks, subs, scale, source_ref, start_ref, core_ref, rows_ref,
                arrived, turned, every, left, total, gram, gram16, whole, basis16,
                part, plane_buf, own_buf, light_buf, image, ysend, yrecv,
                load_sem, own_sem, start_sem, first_send, first_recv, bulk_send, bulk_recv, chunk_send, chunk_recv,
                send1, recv1, send2, recv2, send3, recv3, send4, recv4):
    light = lax.axis_index("light")
    plane = pixes * cams
    pix, cam = lax.axis_index("pix"), lax.axis_index("cam")
    me = pix * cams + cam
    rows, own_cams, width = source_ref.shape
    parts = own_cams // lights
    pieces, piece = turned.shape[1], every.shape[3]
    others = range(lights - 1)
    rank = rows_ref.shape[1]
    height = rows // blocks
    peers = [moved(light, lights, offset) for offset in offsets(lights)]
    light_devices = [{"light": peer} for peer in peers]
    steps = [(offset, turn) for offset in offsets(pixes) + [(0, 0)] for turn in range(cams) if turn or offset != (0, 0)]
    steps.sort(key=lambda step: -(2 * (step[0][0] > 0) + 2 * (step[1] > 0) + step[0][1]))
    plane_devices = [{"pix": moved(pix, pixes, offset), "cam": lax.rem(cam + turn, cams)} for offset, turn in steps]
    plane_peers = [device["pix"] * cams + device["cam"] for device in plane_devices]

    def load(block):
        return pltpu.make_async_copy(
            source_ref.at[pl.ds(block * height, height)], arrived.at[block % 2], load_sem.at[block % 2]
        )

    load(0).start()
    load_start = pltpu.make_async_copy(start_ref, whole, start_sem)
    load_start.start()
    greet(pltpu.get_barrier_semaphore(), plane_devices + light_devices)

    def own_rows(start, size):
        return pl.ds(pl.multiple_of(light * rows + start, 16), size)

    def first_copy(slot, block):
        return pltpu.make_async_remote_copy(
            src_ref=turned.at[peers[slot] * parts, :, pl.ds(block * height, height)],
            dst_ref=every.at[0, :, own_rows(block * height, height)],
            send_sem=first_send.at[slot, block],
            recv_sem=first_recv.at[slot, block],
            device_id=light_devices[slot],
            device_id_type=MESH,
        )


    def bulk_copy(slot):
        return pltpu.make_async_remote_copy(
            src_ref=turned.at[pl.ds(peers[slot] * parts + 1, parts - 2)],
            dst_ref=every.at[pl.ds(1, parts - 2), :, own_rows(0, rows)],
            send_sem=bulk_send.at[slot],
            recv_sem=bulk_recv.at[slot],
            device_id=light_devices[slot],
            device_id_type=MESH,
        )

    def chunk_copy(slot, q):
        return pltpu.make_async_remote_copy(
            src_ref=turned.at[peers[slot] * parts + parts - 1, q],
            dst_ref=every.at[parts - 1, q, own_rows(0, rows)],
            send_sem=chunk_send.at[slot, q],
            recv_sem=chunk_recv.at[slot, q],
            device_id=light_devices[slot],
            device_id_type=MESH,
        )

    def own_copy(part_index):
        return pltpu.make_async_copy(
            turned.at[light * parts + part_index],
            every.at[part_index, :, own_rows(0, rows)],
            own_sem.at[part_index],
        )

    step_rows = 16
    for block in range(blocks):
        if block + 1 < blocks:
            load(block + 1).start()
        load(block).wait()

        def turn(index, carry):
            start = pl.multiple_of(index * step_rows, step_rows)
            some = jnp.transpose(arrived[block % 2, pl.ds(start, step_rows)], (1, 0, 2))
            spot = pl.ds(pl.multiple_of(block * height + start, step_rows), step_rows)
            for q in range(pieces):
                turned[:, q, spot, :] = some[:, :, q * piece : (q + 1) * piece]
            return carry

        lax.fori_loop(0, height // step_rows, turn, 0)
        for slot in reversed(others):
            first_copy(slot, block).start()
    for slot in reversed(others):
        if parts > 2:
            bulk_copy(slot).start()
    for q in range(pieces if parts > 1 else 0):
        for slot in reversed(others):
            chunk_copy(slot, q).start()
    for index in range(parts):
        own_copy(index).start()

    load_start.wait()
    basis = whole[...]
    high = basis.astype(jnp.bfloat16)
    left[:rank] = high.T
    left[rank:] = (basis - high.astype(jnp.float32)).astype(jnp.bfloat16).T
    total[...] = jnp.zeros_like(total)
    gram[...] = jnp.zeros_like(gram)
    for index in range(parts):
        own_copy(index).wait()

    def project(index, q):
        some = every[index, q]
        halves = jnp.dot(left[...], some, preferred_element_type=jnp.float32)
        projected = (halves[:rank] + halves[rank:]).astype(jnp.bfloat16)
        total[...] += lax.dot_general(
            some, projected, (((1,), (1,)), ((), ())), preferred_element_type=jnp.float32
        )

    def correlate(index, q):
        for block in range(lights):
            spot = pl.ds(block * rows, rows)
            gram[spot, :] += lax.dot_general(
                every[index, q, spot], every[index, q], (((1,), (1,)), ((), ())), preferred_element_type=jnp.float32
            )

    def both(chunk, carry):
        index, q = chunk // pieces, lax.rem(chunk, pieces)
        project(index, q)
        correlate(index, q)
        return carry

    last = parts * pieces - 1
    for slot in others:
        for block in range(blocks):
            first_copy(slot, block).wait_recv()
    lax.fori_loop(0, min(pieces, last), both, 0)
    if parts > 2:
        for slot in others:
            bulk_copy(slot).wait_recv()
        lax.fori_loop(pieces, (parts - 1) * pieces, both, 0)
    for q in range(pieces if parts > 1 else 0):
        for slot in others:
            chunk_copy(slot, q).wait_recv()
        if q < pieces - 1:
            both((parts - 1) * pieces + q, 0)
    project(parts - 1, pieces - 1)

    shard = part.shape[1] // plane
    sub_rows = shard // subs

    def shard_rows(index, sub):
        return pl.ds(pl.multiple_of(index * shard + sub * sub_rows, sub_rows), sub_rows)

    def all_reduce(it, fill, meanwhile):
        def copy1(slot, sub):
            return pltpu.make_async_remote_copy(
                src_ref=part.at[it, shard_rows(plane_peers[slot], sub)],
                dst_ref=plane_buf.at[it, slot, sub],
                send_sem=send1.at[it, slot, sub],
                recv_sem=recv1.at[it, slot, sub],
                device_id=plane_devices[slot],
                device_id_type=MESH,
            )

        def copy2(slot, sub):
            return pltpu.make_async_remote_copy(
                src_ref=own_buf.at[it, sub],
                dst_ref=light_buf.at[it, light, sub],
                send_sem=send2.at[it, slot, sub],
                recv_sem=recv2.at[it, slot, sub],
                device_id=light_devices[slot],
                device_id_type=MESH,
            )

        def copy3(slot, sub):
            return pltpu.make_async_remote_copy(
                src_ref=image.at[it, shard_rows(me, sub)],
                dst_ref=image.at[it, shard_rows(me, sub)],
                send_sem=send3.at[it, slot, sub],
                recv_sem=recv3.at[it, slot, sub],
                device_id=plane_devices[slot],
                device_id_type=MESH,
            )

        everyone = range(plane - 1)
        for slot in everyone:
            fill(plane_peers[slot])
            for sub in range(subs):
                copy1(slot, sub).start()
        fill(me)
        meanwhile()
        for sub in range(subs):
            summed = part[it, shard_rows(me, sub), :].astype(jnp.float32)
            for slot in everyone:
                copy1(slot, sub).wait_recv()
                summed += plane_buf[it, slot, sub].astype(jnp.float32)
            own_buf[it, sub] = summed.astype(own_buf.dtype)
            for slot in others:
                copy2(slot, sub).start()
            light_buf[it, light, sub] = summed.astype(own_buf.dtype)
        for sub in range(subs):
            for slot in others:
                copy2(slot, sub).wait_recv()
            summed = light_buf[it, 0, sub].astype(jnp.float32)
            for index in range(1, lights):
                summed += light_buf[it, index, sub].astype(jnp.float32)
            image[it, shard_rows(me, sub), :] = summed.astype(image.dtype)
            for slot in everyone:
                copy3(slot, sub).start()
        for sub in range(subs):
            for slot in everyone:
                copy3(slot, sub).wait_recv()

        def finish():
            for sub in range(subs):
                for slot in everyone:
                    copy1(slot, sub).wait_send()
                    copy3(slot, sub).wait_send()
                for slot in others:
                    copy2(slot, sub).wait_send()

        return finish

    finishes = []
    for it in range(ITERS):
        if it == 0:
            part[it] = (total[...] * scale).astype(part.dtype)

            def meanwhile():
                correlate(parts - 1, pieces - 1)
                gram16[...] = gram[...].astype(jnp.bfloat16)
        else:
            high = basis.astype(jnp.bfloat16)
            basis16[:, :rank] = high
            basis16[:, rank:] = (basis - high.astype(jnp.float32)).astype(jnp.bfloat16)

            def meanwhile():
                pass

        def fill(index):
            if it > 0:
                spot = pl.ds(pl.multiple_of(index * shard, shard), shard)
                halves = jnp.dot(gram16[spot, :], basis16[...], preferred_element_type=jnp.float32)
                part[it, spot] = ((halves[:, :rank] + halves[:, rank:]) * scale).astype(part.dtype)

        finishes.append(all_reduce(it, fill, meanwhile))
        basis = orthonormal(image[it])

    basis16[:, :rank] = basis.astype(jnp.bfloat16)
    share = rank // lights

    def copy4(slot, index):
        return pltpu.make_async_remote_copy(
            src_ref=ysend.at[peers[slot], index],
            dst_ref=yrecv.at[light, index],
            send_sem=send4.at[slot, index],
            recv_sem=recv4.at[slot, index],
            device_id=light_devices[slot],
            device_id_type=MESH,
        )

    for index in range(parts):
        for q in range(pieces):
            y = lax.dot_general(
                basis16[:, :rank], every[index, q], (((0,), (0,)), ((), ())), preferred_element_type=jnp.float32
            ).astype(ysend.dtype)
            for k in range(lights):
                ysend[k, index, q] = y[k * share : (k + 1) * share]
        for slot in others:
            copy4(slot, index).start()
        yrecv[light, index] = ysend[light, index]
    whole[...] = basis
    rows_ref[...] = whole[own_rows(0, rows), :]
    for finish in finishes:
        finish()
    for slot in others:
        for block in range(blocks):
            first_copy(slot, block).wait_send()
        if parts > 2:
            bulk_copy(slot).wait_send()
        for q in range(pieces if parts > 1 else 0):
            chunk_copy(slot, q).wait_send()
    for index in range(parts):
        for slot in others:
            copy4(slot, index).wait_recv()
        for k in range(lights):
            for q in range(pieces):
                core_ref[:, k * parts + index, q * piece : (q + 1) * piece] = yrecv[k, index, q].astype(
                    core_ref.dtype
                )
    for index in range(parts):
        for slot in others:
            copy4(slot, index).wait_send()


def settle_kernel(core_ref, rows_ref, core_out, rows_out, sems):
    copies = [
        pltpu.make_async_copy(core_ref, core_out, sems.at[0]),
        pltpu.make_async_copy(rows_ref, rows_out, sems.at[1]),
    ]
    for copy in copies:
        copy.start()
    for copy in copies:
        copy.wait()


def settle(core, rows):
    vmem, hbm = pl.BlockSpec(memory_space=pltpu.VMEM), pl.BlockSpec(memory_space=pltpu.HBM)
    return pl.pallas_call(
        settle_kernel,
        out_shape=(jax.ShapeDtypeStruct(core.shape, core.dtype), jax.ShapeDtypeStruct(rows.shape, rows.dtype)),
        in_specs=[vmem, vmem],
        out_specs=(hbm, hbm),
        scratch_shapes=[pltpu.SemaphoreType.DMA((2,))],
        compiler_params=pltpu.CompilerParams(vmem_limit_bytes=8 * 1024 * 1024),
    )(core, rows)


def per_device(reflectance, start_basis):
    rows, own_cams, width = reflectance.shape
    rank = start_basis.shape[1]
    lights, pixes, cams = (lax.axis_size(name) for name in ("light", "pix", "cam"))
    plane = pixes * cams
    all_rows, share, parts = rows * lights, rank // lights, own_cams // lights
    scale = 1.0 / (own_cams * width * cams * pixes)
    piece = min(256, width)
    pieces = width // piece
    blocks = max(1, rows // 64)
    shard = all_rows // plane
    subs = 2
    vmem, hbm = pl.BlockSpec(memory_space=pltpu.VMEM), pl.BlockSpec(memory_space=pltpu.HBM)
    dma = pltpu.SemaphoreType.DMA
    bf16, f32 = jnp.bfloat16, jnp.float32
    sub_shape = (subs, shard // subs, rank)
    core, basis_rows = pl.pallas_call(
        functools.partial(step_kernel, lights, pixes, cams, blocks, subs, scale),
        out_shape=(
            jax.ShapeDtypeStruct((share, own_cams, width), f32),
            jax.ShapeDtypeStruct((rows, rank), f32),
        ),
        in_specs=[hbm, hbm],
        out_specs=(vmem, vmem),
        scratch_shapes=[
            pltpu.VMEM((2, rows // blocks, own_cams, width), bf16),
            pltpu.VMEM((own_cams, pieces, rows, piece), bf16),
            pltpu.VMEM((parts, pieces, all_rows, piece), bf16),
            pltpu.VMEM((2 * rank, all_rows), bf16),
            pltpu.VMEM((all_rows, rank), f32),
            pltpu.VMEM((all_rows, all_rows), f32),
            pltpu.VMEM((all_rows, all_rows), bf16),
            pltpu.VMEM((all_rows, rank), f32),
            pltpu.VMEM((all_rows, 2 * rank), bf16),
            pltpu.VMEM((ITERS, all_rows, rank), bf16),
            pltpu.VMEM((ITERS, plane - 1) + sub_shape, bf16),
            pltpu.VMEM((ITERS,) + sub_shape, bf16),
            pltpu.VMEM((ITERS, lights) + sub_shape, bf16),
            pltpu.VMEM((ITERS, all_rows, rank), bf16),
            pltpu.VMEM((lights, parts, pieces, share, piece), bf16),
            pltpu.VMEM((lights, parts, pieces, share, piece), bf16),
            dma((2,)), dma((parts,)), dma,
            dma((lights - 1, blocks)), dma((lights - 1, blocks)),
            dma((lights - 1,)), dma((lights - 1,)), dma((lights - 1, pieces)), dma((lights - 1, pieces)),
            dma((ITERS, plane - 1, subs)), dma((ITERS, plane - 1, subs)),
            dma((ITERS, lights - 1, subs)), dma((ITERS, lights - 1, subs)),
            dma((ITERS, plane - 1, subs)), dma((ITERS, plane - 1, subs)),
            dma((lights - 1, parts)), dma((lights - 1, parts)),
        ],
        compiler_params=pltpu.CompilerParams(
            collective_id=0, has_side_effects=True, vmem_limit_bytes=44 * 1024 * 1024
        ),
    )(reflectance, pltpu.with_memory_space_constraint(start_basis, pltpu.HBM))
    return settle(core, basis_rows)


def solution(mesh):
    return jax.shard_map(
        per_device,
        mesh=mesh,
        in_specs=(P("light", "cam", "pix"), P()),
        out_specs=(P("light", "cam", "pix"), P("light", None)),
        check_vma=False,
    )
```

```python
import functools

import jax
import jax.numpy as jnp
from jax import lax
from jax.experimental import pallas as pl
from jax.experimental.pallas import tpu as pltpu
from jax.sharding import PartitionSpec as P

ITERS = 2
MESH = pl.DeviceIdType.MESH


def greet(barrier, devices):
    for device in devices:
        pl.semaphore_signal(barrier, inc=1, device_id=device, device_id_type=MESH)
    pl.semaphore_wait(barrier, len(devices))


def offsets(count):
    even = range(0, count, 2)
    return [(turn, swap) for turn in reversed(even) for swap in (1, 0) if turn or swap]


def moved(place, count, offset):
    turn, swap = offset
    there = lax.rem(place + turn, count)
    return there + (1 - 2 * lax.rem(there, 2)) if swap else there


def triangular_inverse(inner):
    rank = inner.shape[0]
    height = 8
    shape = (height, rank)
    sub = lax.broadcasted_iota(jnp.int32, shape, 0)
    lane = lax.broadcasted_iota(jnp.int32, shape, 1)
    count = rank // height
    left = [inner[height * t : height * (t + 1), :] for t in range(count)]
    right = [jnp.where(lane == sub + height * t, 1.0, 0.0) for t in range(count)]

    def spread_row(tile, k):
        return jnp.broadcast_to(tile[k : k + 1, :], shape)

    def spread_column(tile, j):
        return jnp.broadcast_to(tile[:, j : j + 1], shape)

    columns = [spread_column(left[0], k) for k in range(height)]
    for p in range(count):
        first = height * p
        top, below, jordan = left[p], right[p], right[p]
        ahead, own, base = [], [], []
        if p + 1 < count:
            ahead = [spread_column(top, first + height + k) for k in range(height)]
            own = [spread_column(left[p + 1], first + k) for k in range(height)]
            base = [spread_column(left[p + 1], first + height + k) for k in range(height)]
        pivots, inverses = jnp.ones(shape, jnp.float32), jnp.ones(shape, jnp.float32)
        for k in range(height):
            pivot = spread_row(columns[k], k)
            inverse = 1.0 / pivot
            pivots = jnp.where(sub == k, pivot, pivots)
            inverses = jnp.where(sub == k, inverse, inverses)
            factor = columns[k] * inverse
            down = jnp.where(sub > k, factor, 0.0)
            factor = jnp.where(sub != k, factor, 0.0)
            for later in range(k + 1, height):
                columns[later] = columns[later] - factor * spread_row(columns[later], k)
            ahead = [column - factor * spread_row(column, k) for column in ahead]
            top = top - factor * spread_row(top, k)
            jordan = jordan - factor * spread_row(jordan, k)
            below = below - down * spread_row(below, k)
        right[p] = below * lax.rsqrt(pivots)
        if p + 1 == count:
            break
        top, jordan = top * inverses, jordan * inverses
        columns = []
        for k in range(height):
            scaled, column = ahead[k] * inverses, base[k]
            for j in range(height):
                column = column - own[j] * spread_row(scaled, j)
            columns.append(column)
        top_rows = [spread_row(top, k) for k in range(height)]
        below_rows = [spread_row(jordan, k) for k in range(height)]
        for t in range(p + 1, count):
            side = own if t == p + 1 else [spread_column(left[t], first + k) for k in range(height)]
            upper, lower = left[t], right[t]
            for k in range(height):
                upper = upper - side[k] * top_rows[k]
                lower = lower - side[k] * below_rows[k]
            left[t], right[t] = upper, lower
    return jnp.concatenate(right, axis=0)


def orthonormal(image):
    inner = lax.dot_general(image, image, (((0,), (0,)), ((), ())), preferred_element_type=jnp.float32)
    inverse = triangular_inverse(inner)
    high = inverse.astype(jnp.bfloat16)
    low = (inverse - high.astype(jnp.float32)).astype(jnp.bfloat16)
    return lax.dot_general(
        jnp.concatenate([image, image], axis=1), jnp.concatenate([high, low], axis=1),
        (((1,), (1,)), ((), ())), preferred_element_type=jnp.float32,
    )


def step_kernel(lights, pixes, cams, blocks, subs, scale, source_ref, start_ref, core_ref, rows_ref,
                arrived, turned, every, left, total, gram, gram16, whole, basis16,
                part, plane_buf, own_buf, light_buf, image, ysend, yrecv,
                load_sem, own_sem, start_sem, first_send, first_recv, bulk_send, bulk_recv, chunk_send, chunk_recv,
                send1, recv1, send2, recv2, send3, recv3, send4, recv4):
    light = lax.axis_index("light")
    plane = pixes * cams
    pix, cam = lax.axis_index("pix"), lax.axis_index("cam")
    me = pix * cams + cam
    rows, own_cams, width = source_ref.shape
    parts = own_cams // lights
    pieces, piece = turned.shape[1], every.shape[3]
    others = range(lights - 1)
    rank = rows_ref.shape[1]
    height = rows // blocks
    peers = [moved(light, lights, offset) for offset in offsets(lights)]
    light_devices = [{"light": peer} for peer in peers]
    steps = [(offset, turn) for offset in offsets(pixes) + [(0, 0)] for turn in range(cams) if turn or offset != (0, 0)]
    steps.sort(key=lambda step: -(2 * (step[0][0] > 0) + 2 * (step[1] > 0) + step[0][1]))
    plane_devices = [{"pix": moved(pix, pixes, offset), "cam": lax.rem(cam + turn, cams)} for offset, turn in steps]
    plane_peers = [device["pix"] * cams + device["cam"] for device in plane_devices]

    def load(block):
        return pltpu.make_async_copy(
            source_ref.at[pl.ds(block * height, height)], arrived.at[block % 2], load_sem.at[block % 2]
        )

    load(0).start()
    load_start = pltpu.make_async_copy(start_ref, whole, start_sem)
    load_start.start()
    greet(pltpu.get_barrier_semaphore(), light_devices + plane_devices)

    def own_rows(start, size):
        return pl.ds(pl.multiple_of(light * rows + start, 16), size)

    def first_copy(slot, block):
        return pltpu.make_async_remote_copy(
            src_ref=turned.at[peers[slot] * parts, :, pl.ds(block * height, height)],
            dst_ref=every.at[0, :, own_rows(block * height, height)],
            send_sem=first_send.at[slot, block],
            recv_sem=first_recv.at[slot, block],
            device_id=light_devices[slot],
            device_id_type=MESH,
        )


    def bulk_copy(slot):
        return pltpu.make_async_remote_copy(
            src_ref=turned.at[pl.ds(peers[slot] * parts + 1, parts - 2)],
            dst_ref=every.at[pl.ds(1, parts - 2), :, own_rows(0, rows)],
            send_sem=bulk_send.at[slot],
            recv_sem=bulk_recv.at[slot],
            device_id=light_devices[slot],
            device_id_type=MESH,
        )

    def chunk_copy(slot, q):
        return pltpu.make_async_remote_copy(
            src_ref=turned.at[peers[slot] * parts + parts - 1, q],
            dst_ref=every.at[parts - 1, q, own_rows(0, rows)],
            send_sem=chunk_send.at[slot, q],
            recv_sem=chunk_recv.at[slot, q],
            device_id=light_devices[slot],
            device_id_type=MESH,
        )

    def own_copy(part_index):
        return pltpu.make_async_copy(
            turned.at[light * parts + part_index],
            every.at[part_index, :, own_rows(0, rows)],
            own_sem.at[part_index],
        )

    step_rows = 16
    for block in range(blocks):
        if block + 1 < blocks:
            load(block + 1).start()
        load(block).wait()

        def turn(index, carry):
            start = pl.multiple_of(index * step_rows, step_rows)
            some = jnp.transpose(arrived[block % 2, pl.ds(start, step_rows)], (1, 0, 2))
            spot = pl.ds(pl.multiple_of(block * height + start, step_rows), step_rows)
            for q in range(pieces):
                turned[:, q, spot, :] = some[:, :, q * piece : (q + 1) * piece]
            return carry

        lax.fori_loop(0, height // step_rows, turn, 0)
        for slot in reversed(others):
            first_copy(slot, block).start()
    for slot in reversed(others):
        if parts > 2:
            bulk_copy(slot).start()
    for q in range(pieces if parts > 1 else 0):
        for slot in reversed(others):
            chunk_copy(slot, q).start()
    for index in range(parts):
        own_copy(index).start()

    load_start.wait()
    basis = whole[...]
    high = basis.astype(jnp.bfloat16)
    left[:rank] = high.T
    left[rank:] = (basis - high.astype(jnp.float32)).astype(jnp.bfloat16).T
    total[...] = jnp.zeros_like(total)
    gram[...] = jnp.zeros_like(gram)
    for index in range(parts):
        own_copy(index).wait()

    def project(index, q):
        some = every[index, q]
        halves = jnp.dot(left[...], some, preferred_element_type=jnp.float32)
        projected = (halves[:rank] + halves[rank:]).astype(jnp.bfloat16)
        total[...] += lax.dot_general(
            some, projected, (((1,), (1,)), ((), ())), preferred_element_type=jnp.float32
        )

    def correlate(index, q):
        for block in range(lights):
            spot = pl.ds(block * rows, rows)
            gram[spot, :] += lax.dot_general(
                every[index, q, spot], every[index, q], (((1,), (1,)), ((), ())), preferred_element_type=jnp.float32
            )

    def both(chunk, carry):
        index, q = chunk // pieces, lax.rem(chunk, pieces)
        project(index, q)
        correlate(index, q)
        return carry

    last = parts * pieces - 1
    for slot in others:
        for block in range(blocks):
            first_copy(slot, block).wait_recv()
    lax.fori_loop(0, min(pieces, last), both, 0)
    if parts > 2:
        for slot in others:
            bulk_copy(slot).wait_recv()
        lax.fori_loop(pieces, (parts - 1) * pieces, both, 0)
    for q in range(pieces if parts > 1 else 0):
        for slot in others:
            chunk_copy(slot, q).wait_recv()
        if q < pieces - 1:
            both((parts - 1) * pieces + q, 0)
    project(parts - 1, pieces - 1)

    shard = part.shape[1] // plane
    sub_rows = shard // subs

    def shard_rows(index, sub):
        return pl.ds(pl.multiple_of(index * shard + sub * sub_rows, sub_rows), sub_rows)

    def all_reduce(it, fill, meanwhile):
        def copy1(slot, sub):
            return pltpu.make_async_remote_copy(
                src_ref=part.at[it, shard_rows(plane_peers[slot], sub)],
                dst_ref=plane_buf.at[it, slot, sub],
                send_sem=send1.at[it, slot, sub],
                recv_sem=recv1.at[it, slot, sub],
                device_id=plane_devices[slot],
                device_id_type=MESH,
            )

        def copy2(slot, sub):
            return pltpu.make_async_remote_copy(
                src_ref=own_buf.at[it, sub],
                dst_ref=light_buf.at[it, light, sub],
                send_sem=send2.at[it, slot, sub],
                recv_sem=recv2.at[it, slot, sub],
                device_id=light_devices[slot],
                device_id_type=MESH,
            )

        def copy3(slot, sub):
            return pltpu.make_async_remote_copy(
                src_ref=image.at[it, shard_rows(me, sub)],
                dst_ref=image.at[it, shard_rows(me, sub)],
                send_sem=send3.at[it, slot, sub],
                recv_sem=recv3.at[it, slot, sub],
                device_id=plane_devices[slot],
                device_id_type=MESH,
            )

        everyone = range(plane - 1)
        for slot in everyone:
            fill(plane_peers[slot])
            for sub in range(subs):
                copy1(slot, sub).start()
        fill(me)
        meanwhile()
        for sub in range(subs):
            summed = part[it, shard_rows(me, sub), :].astype(jnp.float32)
            for slot in everyone:
                copy1(slot, sub).wait_recv()
                summed += plane_buf[it, slot, sub].astype(jnp.float32)
            own_buf[it, sub] = summed.astype(own_buf.dtype)
            for slot in others:
                copy2(slot, sub).start()
            light_buf[it, light, sub] = summed.astype(own_buf.dtype)
        for sub in range(subs):
            for slot in others:
                copy2(slot, sub).wait_recv()
            summed = light_buf[it, 0, sub].astype(jnp.float32)
            for index in range(1, lights):
                summed += light_buf[it, index, sub].astype(jnp.float32)
            image[it, shard_rows(me, sub), :] = summed.astype(image.dtype)
            for slot in everyone:
                copy3(slot, sub).start()
        for sub in range(subs):
            for slot in everyone:
                copy3(slot, sub).wait_recv()

        def finish():
            for sub in range(subs):
                for slot in everyone:
                    copy1(slot, sub).wait_send()
                    copy3(slot, sub).wait_send()
                for slot in others:
                    copy2(slot, sub).wait_send()

        return finish

    finishes = []
    for it in range(ITERS):
        if it == 0:
            def meanwhile():
                correlate(parts - 1, pieces - 1)
                gram16[...] = gram[...].astype(jnp.bfloat16)
        else:
            high = basis.astype(jnp.bfloat16)
            basis16[:, :rank] = high
            basis16[:, rank:] = (basis - high.astype(jnp.float32)).astype(jnp.bfloat16)

            def meanwhile():
                pass

        def fill(index):
            spot = pl.ds(pl.multiple_of(index * shard, shard), shard)
            if it == 0:
                part[it, spot] = (total[spot, :] * scale).astype(part.dtype)
            else:
                halves = jnp.dot(gram16[spot, :], basis16[...], preferred_element_type=jnp.float32)
                part[it, spot] = ((halves[:, :rank] + halves[:, rank:]) * scale).astype(part.dtype)

        finishes.append(all_reduce(it, fill, meanwhile))
        basis = orthonormal(image[it])

    left[:rank] = basis.astype(jnp.bfloat16).T
    share = rank // lights

    def copy4(slot, index):
        return pltpu.make_async_remote_copy(
            src_ref=ysend.at[peers[slot], index],
            dst_ref=yrecv.at[light, index],
            send_sem=send4.at[slot, index],
            recv_sem=recv4.at[slot, index],
            device_id=light_devices[slot],
            device_id_type=MESH,
        )

    for index in range(parts):
        for q in range(pieces):
            y = jnp.dot(left[:rank], every[index, q], preferred_element_type=jnp.float32).astype(ysend.dtype)
            for k in range(lights):
                ysend[k, index, q] = y[k * share : (k + 1) * share]
        for slot in reversed(others):
            copy4(slot, index).start()
        yrecv[light, index] = ysend[light, index]
    whole[...] = basis
    rows_ref[...] = whole[own_rows(0, rows), :]
    for finish in finishes:
        finish()
    for slot in others:
        for block in range(blocks):
            first_copy(slot, block).wait_send()
        if parts > 2:
            bulk_copy(slot).wait_send()
        for q in range(pieces if parts > 1 else 0):
            chunk_copy(slot, q).wait_send()
    for index in range(parts):
        for slot in others:
            copy4(slot, index).wait_recv()
        for k in range(lights):
            for q in range(pieces):
                core_ref[:, k * parts + index, q * piece : (q + 1) * piece] = yrecv[k, index, q].astype(
                    core_ref.dtype
                )
    for index in range(parts):
        for slot in others:
            copy4(slot, index).wait_send()


def settle_kernel(core_ref, rows_ref, core_out, rows_out, sems):
    copies = [
        pltpu.make_async_copy(core_ref, core_out, sems.at[0]),
        pltpu.make_async_copy(rows_ref, rows_out, sems.at[1]),
    ]
    for copy in copies:
        copy.start()
    for copy in copies:
        copy.wait()


def settle(core, rows):
    vmem, hbm = pl.BlockSpec(memory_space=pltpu.VMEM), pl.BlockSpec(memory_space=pltpu.HBM)
    return pl.pallas_call(
        settle_kernel,
        out_shape=(jax.ShapeDtypeStruct(core.shape, core.dtype), jax.ShapeDtypeStruct(rows.shape, rows.dtype)),
        in_specs=[vmem, vmem],
        out_specs=(hbm, hbm),
        scratch_shapes=[pltpu.SemaphoreType.DMA((2,))],
        compiler_params=pltpu.CompilerParams(vmem_limit_bytes=8 * 1024 * 1024),
    )(core, rows)


def per_device(reflectance, start_basis):
    rows, own_cams, width = reflectance.shape
    rank = start_basis.shape[1]
    lights, pixes, cams = (lax.axis_size(name) for name in ("light", "pix", "cam"))
    plane = pixes * cams
    all_rows, share, parts = rows * lights, rank // lights, own_cams // lights
    scale = 1.0 / (own_cams * width * cams * pixes)
    piece = min(256, width)
    pieces = width // piece
    blocks = max(1, rows // 64)
    shard = all_rows // plane
    subs = 2
    vmem, hbm = pl.BlockSpec(memory_space=pltpu.VMEM), pl.BlockSpec(memory_space=pltpu.HBM)
    dma = pltpu.SemaphoreType.DMA
    bf16, f32 = jnp.bfloat16, jnp.float32
    sub_shape = (subs, shard // subs, rank)
    core, basis_rows = pl.pallas_call(
        functools.partial(step_kernel, lights, pixes, cams, blocks, subs, scale),
        out_shape=(
            jax.ShapeDtypeStruct((share, own_cams, width), f32),
            jax.ShapeDtypeStruct((rows, rank), f32),
        ),
        in_specs=[hbm, hbm],
        out_specs=(vmem, vmem),
        scratch_shapes=[
            pltpu.VMEM((2, rows // blocks, own_cams, width), bf16),
            pltpu.VMEM((own_cams, pieces, rows, piece), bf16),
            pltpu.VMEM((parts, pieces, all_rows, piece), bf16),
            pltpu.VMEM((2 * rank, all_rows), bf16),
            pltpu.VMEM((all_rows, rank), f32),
            pltpu.VMEM((all_rows, all_rows), f32),
            pltpu.VMEM((all_rows, all_rows), bf16),
            pltpu.VMEM((all_rows, rank), f32),
            pltpu.VMEM((all_rows, 2 * rank), bf16),
            pltpu.VMEM((ITERS, all_rows, rank), bf16),
            pltpu.VMEM((ITERS, plane - 1) + sub_shape, bf16),
            pltpu.VMEM((ITERS,) + sub_shape, bf16),
            pltpu.VMEM((ITERS, lights) + sub_shape, bf16),
            pltpu.VMEM((ITERS, all_rows, rank), bf16),
            pltpu.VMEM((lights, parts, pieces, share, piece), bf16),
            pltpu.VMEM((lights, parts, pieces, share, piece), bf16),
            dma((2,)), dma((parts,)), dma,
            dma((lights - 1, blocks)), dma((lights - 1, blocks)),
            dma((lights - 1,)), dma((lights - 1,)), dma((lights - 1, pieces)), dma((lights - 1, pieces)),
            dma((ITERS, plane - 1, subs)), dma((ITERS, plane - 1, subs)),
            dma((ITERS, lights - 1, subs)), dma((ITERS, lights - 1, subs)),
            dma((ITERS, plane - 1, subs)), dma((ITERS, plane - 1, subs)),
            dma((lights - 1, parts)), dma((lights - 1, parts)),
        ],
        compiler_params=pltpu.CompilerParams(
            collective_id=0, has_side_effects=True, vmem_limit_bytes=44 * 1024 * 1024
        ),
    )(reflectance, pltpu.with_memory_space_constraint(start_basis, pltpu.HBM))
    return settle(core, basis_rows)


def solution(mesh):
    return jax.shard_map(
        per_device,
        mesh=mesh,
        in_specs=(P("light", "cam", "pix"), P()),
        out_specs=(P("light", "cam", "pix"), P("light", None)),
        check_vma=False,
    )
```

```python
import functools

import jax
import jax.numpy as jnp
from jax import lax
from jax.experimental import pallas as pl
from jax.experimental.pallas import tpu as pltpu
from jax.sharding import PartitionSpec as P

ITERS = 2
MESH = pl.DeviceIdType.MESH


def greet(barrier, devices):
    for device in devices:
        pl.semaphore_signal(barrier, inc=1, device_id=device, device_id_type=MESH)
    pl.semaphore_wait(barrier, len(devices))


def offsets(count):
    even = range(0, count, 2)
    return [(turn, swap) for turn in reversed(even) for swap in (1, 0) if turn or swap]


def moved(place, count, offset):
    turn, swap = offset
    there = lax.rem(place + turn, count)
    return there + (1 - 2 * lax.rem(there, 2)) if swap else there


def triangular_inverse(inner):
    rank = inner.shape[0]
    height = 8
    shape = (height, rank)
    sub = lax.broadcasted_iota(jnp.int32, shape, 0)
    lane = lax.broadcasted_iota(jnp.int32, shape, 1)
    count = rank // height
    left = [inner[height * t : height * (t + 1), :] for t in range(count)]
    right = [jnp.where(lane == sub + height * t, 1.0, 0.0) for t in range(count)]

    def spread_row(tile, k):
        return jnp.broadcast_to(tile[k : k + 1, :], shape)

    def spread_column(tile, j):
        return jnp.broadcast_to(tile[:, j : j + 1], shape)

    columns = [spread_column(left[0], k) for k in range(height)]
    for p in range(count):
        first = height * p
        top, below, jordan = left[p], right[p], right[p]
        ahead, own, base = [], [], []
        if p + 1 < count:
            ahead = [spread_column(top, first + height + k) for k in range(height)]
            own = [spread_column(left[p + 1], first + k) for k in range(height)]
            base = [spread_column(left[p + 1], first + height + k) for k in range(height)]
        pivots, inverses = jnp.ones(shape, jnp.float32), jnp.ones(shape, jnp.float32)
        for k in range(height):
            pivot = spread_row(columns[k], k)
            inverse = 1.0 / pivot
            pivots = jnp.where(sub == k, pivot, pivots)
            inverses = jnp.where(sub == k, inverse, inverses)
            factor = columns[k] * inverse
            down = jnp.where(sub > k, factor, 0.0)
            factor = jnp.where(sub != k, factor, 0.0)
            for later in range(k + 1, height):
                columns[later] = columns[later] - factor * spread_row(columns[later], k)
            ahead = [column - factor * spread_row(column, k) for column in ahead]
            top = top - factor * spread_row(top, k)
            jordan = jordan - factor * spread_row(jordan, k)
            below = below - down * spread_row(below, k)
        right[p] = below * lax.rsqrt(pivots)
        if p + 1 == count:
            break
        top, jordan = top * inverses, jordan * inverses
        columns = []
        for k in range(height):
            scaled, column = ahead[k] * inverses, base[k]
            for j in range(height):
                column = column - own[j] * spread_row(scaled, j)
            columns.append(column)
        top_rows = [spread_row(top, k) for k in range(height)]
        below_rows = [spread_row(jordan, k) for k in range(height)]
        for t in range(p + 1, count):
            side = own if t == p + 1 else [spread_column(left[t], first + k) for k in range(height)]
            upper, lower = left[t], right[t]
            for k in range(height):
                upper = upper - side[k] * top_rows[k]
                lower = lower - side[k] * below_rows[k]
            left[t], right[t] = upper, lower
    return jnp.concatenate(right, axis=0)


def orthonormal(image):
    inner = lax.dot_general(image, image, (((0,), (0,)), ((), ())), preferred_element_type=jnp.float32)
    inverse = triangular_inverse(inner)
    high = inverse.astype(jnp.bfloat16)
    low = (inverse - high.astype(jnp.float32)).astype(jnp.bfloat16)
    return lax.dot_general(
        jnp.concatenate([image, image], axis=1), jnp.concatenate([high, low], axis=1),
        (((1,), (1,)), ((), ())), preferred_element_type=jnp.float32,
    )


def step_kernel(lights, pixes, cams, blocks, subs, scale, source_ref, start_ref, core_ref, rows_ref,
                arrived, turned, every, left, total, gram, gram16, whole, basis16,
                part, plane_buf, own_buf, light_buf, image, ysend, yrecv,
                load_sem, own_sem, start_sem, first_send, first_recv, bulk_send, bulk_recv, chunk_send, chunk_recv,
                send1, recv1, send2, recv2, send3, recv3, send4, recv4):
    light = lax.axis_index("light")
    plane = pixes * cams
    pix, cam = lax.axis_index("pix"), lax.axis_index("cam")
    me = pix * cams + cam
    rows, own_cams, width = source_ref.shape
    parts = own_cams // lights
    pieces, piece = turned.shape[1], every.shape[3]
    others = range(lights - 1)
    rank = rows_ref.shape[1]
    height = rows // blocks
    peers = [moved(light, lights, offset) for offset in offsets(lights)]
    light_devices = [{"light": peer} for peer in peers]
    steps = [(offset, turn) for offset in offsets(pixes) + [(0, 0)] for turn in range(cams) if turn or offset != (0, 0)]
    steps.sort(key=lambda step: -(2 * (step[0][0] > 0) + 2 * (step[1] > 0) + step[0][1]))
    plane_devices = [{"pix": moved(pix, pixes, offset), "cam": lax.rem(cam + turn, cams)} for offset, turn in steps]
    plane_peers = [device["pix"] * cams + device["cam"] for device in plane_devices]

    def load(block):
        return pltpu.make_async_copy(
            source_ref.at[pl.ds(block * height, height)], arrived.at[block % 2], load_sem.at[block % 2]
        )

    load(0).start()
    load_start = pltpu.make_async_copy(start_ref, whole, start_sem)
    load_start.start()
    greet(pltpu.get_barrier_semaphore(), light_devices + plane_devices)

    def own_rows(start, size):
        return pl.ds(pl.multiple_of(light * rows + start, 16), size)

    def first_copy(slot, block):
        return pltpu.make_async_remote_copy(
            src_ref=turned.at[peers[slot] * parts, :, pl.ds(block * height, height)],
            dst_ref=every.at[0, :, own_rows(block * height, height)],
            send_sem=first_send.at[slot, block],
            recv_sem=first_recv.at[slot, block],
            device_id=light_devices[slot],
            device_id_type=MESH,
        )


    def bulk_copy(slot):
        return pltpu.make_async_remote_copy(
            src_ref=turned.at[pl.ds(peers[slot] * parts + 1, parts - 2)],
            dst_ref=every.at[pl.ds(1, parts - 2), :, own_rows(0, rows)],
            send_sem=bulk_send.at[slot],
            recv_sem=bulk_recv.at[slot],
            device_id=light_devices[slot],
            device_id_type=MESH,
        )

    def chunk_copy(slot, q):
        return pltpu.make_async_remote_copy(
            src_ref=turned.at[peers[slot] * parts + parts - 1, q],
            dst_ref=every.at[parts - 1, q, own_rows(0, rows)],
            send_sem=chunk_send.at[slot, q],
            recv_sem=chunk_recv.at[slot, q],
            device_id=light_devices[slot],
            device_id_type=MESH,
        )

    def own_copy(part_index):
        return pltpu.make_async_copy(
            turned.at[light * parts + part_index],
            every.at[part_index, :, own_rows(0, rows)],
            own_sem.at[part_index],
        )

    step_rows = 16
    for block in range(blocks):
        if block + 1 < blocks:
            load(block + 1).start()
        load(block).wait()

        def turn(index, carry):
            start = pl.multiple_of(index * step_rows, step_rows)
            some = jnp.transpose(arrived[block % 2, pl.ds(start, step_rows)], (1, 0, 2))
            spot = pl.ds(pl.multiple_of(block * height + start, step_rows), step_rows)
            for q in range(pieces):
                turned[:, q, spot, :] = some[:, :, q * piece : (q + 1) * piece]
            return carry

        lax.fori_loop(0, height // step_rows, turn, 0)
        for slot in reversed(others):
            first_copy(slot, block).start()
    for slot in reversed(others):
        if parts > 2:
            bulk_copy(slot).start()
    for q in range(pieces if parts > 1 else 0):
        for slot in reversed(others):
            chunk_copy(slot, q).start()
    for index in range(parts):
        own_copy(index).start()

    load_start.wait()
    basis = whole[...]
    high = basis.astype(jnp.bfloat16)
    left[:rank] = high.T
    left[rank:] = (basis - high.astype(jnp.float32)).astype(jnp.bfloat16).T
    total[...] = jnp.zeros_like(total)
    gram[...] = jnp.zeros_like(gram)
    for index in range(parts):
        own_copy(index).wait()

    def projection(index, q):
        halves = jnp.dot(left[...], every[index, q], preferred_element_type=jnp.float32)
        return (halves[:rank] + halves[rank:]).astype(jnp.bfloat16)

    def project(index, q):
        total[...] += lax.dot_general(
            every[index, q], projection(index, q), (((1,), (1,)), ((), ())), preferred_element_type=jnp.float32
        )

    def correlate(index, q):
        for block in range(lights):
            spot = pl.ds(block * rows, rows)
            gram[spot, :] += lax.dot_general(
                every[index, q, spot], every[index, q], (((1,), (1,)), ((), ())), preferred_element_type=jnp.float32
            )

    def both(chunk, carry):
        index, q = chunk // pieces, lax.rem(chunk, pieces)
        project(index, q)
        correlate(index, q)
        return carry

    last = parts * pieces - 1
    for slot in others:
        for block in range(blocks):
            first_copy(slot, block).wait_recv()
    lax.fori_loop(0, min(pieces, last), both, 0)
    if parts > 2:
        for slot in others:
            bulk_copy(slot).wait_recv()
        lax.fori_loop(pieces, (parts - 1) * pieces, both, 0)
    for q in range(pieces if parts > 1 else 0):
        for slot in others:
            chunk_copy(slot, q).wait_recv()
        if q < pieces - 1:
            both((parts - 1) * pieces + q, 0)
    projected = projection(parts - 1, pieces - 1)

    shard = part.shape[1] // plane
    sub_rows = shard // subs

    def shard_rows(index, sub):
        return pl.ds(pl.multiple_of(index * shard + sub * sub_rows, sub_rows), sub_rows)

    def all_reduce(it, fill, meanwhile):
        def copy1(slot, sub):
            return pltpu.make_async_remote_copy(
                src_ref=part.at[it, shard_rows(plane_peers[slot], sub)],
                dst_ref=plane_buf.at[it, slot, sub],
                send_sem=send1.at[it, slot, sub],
                recv_sem=recv1.at[it, slot, sub],
                device_id=plane_devices[slot],
                device_id_type=MESH,
            )

        def copy2(slot, sub):
            return pltpu.make_async_remote_copy(
                src_ref=own_buf.at[it, sub],
                dst_ref=light_buf.at[it, light, sub],
                send_sem=send2.at[it, slot, sub],
                recv_sem=recv2.at[it, slot, sub],
                device_id=light_devices[slot],
                device_id_type=MESH,
            )

        def copy3(slot, sub):
            return pltpu.make_async_remote_copy(
                src_ref=image.at[it, shard_rows(me, sub)],
                dst_ref=image.at[it, shard_rows(me, sub)],
                send_sem=send3.at[it, slot, sub],
                recv_sem=recv3.at[it, slot, sub],
                device_id=plane_devices[slot],
                device_id_type=MESH,
            )

        everyone = range(plane - 1)
        for slot in everyone:
            fill(plane_peers[slot])
            for sub in range(subs):
                copy1(slot, sub).start()
        fill(me)
        meanwhile()
        for sub in range(subs):
            summed = part[it, shard_rows(me, sub), :].astype(jnp.float32)
            for slot in everyone:
                copy1(slot, sub).wait_recv()
                summed += plane_buf[it, slot, sub].astype(jnp.float32)
            own_buf[it, sub] = summed.astype(own_buf.dtype)
            for slot in others:
                copy2(slot, sub).start()
            light_buf[it, light, sub] = summed.astype(own_buf.dtype)
        for sub in range(subs):
            for slot in others:
                copy2(slot, sub).wait_recv()
            summed = light_buf[it, 0, sub].astype(jnp.float32)
            for index in range(1, lights):
                summed += light_buf[it, index, sub].astype(jnp.float32)
            image[it, shard_rows(me, sub), :] = summed.astype(image.dtype)
            for slot in everyone:
                copy3(slot, sub).start()
        for sub in range(subs):
            for slot in everyone:
                copy3(slot, sub).wait_recv()

        def finish():
            for sub in range(subs):
                for slot in everyone:
                    copy1(slot, sub).wait_send()
                    copy3(slot, sub).wait_send()
                for slot in others:
                    copy2(slot, sub).wait_send()

        return finish

    finishes = []
    for it in range(ITERS):
        if it == 0:
            def meanwhile():
                correlate(parts - 1, pieces - 1)
                gram16[...] = gram[...].astype(jnp.bfloat16)
        else:
            high = basis.astype(jnp.bfloat16)
            basis16[:, :rank] = high
            basis16[:, rank:] = (basis - high.astype(jnp.float32)).astype(jnp.bfloat16)

            def meanwhile():
                pass

        def fill(index):
            spot = pl.ds(pl.multiple_of(index * shard, shard), shard)
            if it == 0:
                product = lax.dot_general(
                    every[parts - 1, pieces - 1, spot], projected, (((1,), (1,)), ((), ())),
                    preferred_element_type=jnp.float32,
                )
                part[it, spot] = ((total[spot, :] + product) * scale).astype(part.dtype)
            else:
                halves = jnp.dot(gram16[spot, :], basis16[...], preferred_element_type=jnp.float32)
                part[it, spot] = ((halves[:, :rank] + halves[:, rank:]) * scale).astype(part.dtype)

        finishes.append(all_reduce(it, fill, meanwhile))
        basis = orthonormal(image[it])

    left[:rank] = basis.astype(jnp.bfloat16).T
    share = rank // lights

    def copy4(slot, index):
        return pltpu.make_async_remote_copy(
            src_ref=ysend.at[peers[slot], index],
            dst_ref=yrecv.at[light, index],
            send_sem=send4.at[slot, index],
            recv_sem=recv4.at[slot, index],
            device_id=light_devices[slot],
            device_id_type=MESH,
        )

    for index in range(parts):
        for q in range(pieces):
            y = jnp.dot(left[:rank], every[index, q], preferred_element_type=jnp.float32).astype(ysend.dtype)
            for k in range(lights):
                ysend[k, index, q] = y[k * share : (k + 1) * share]
        for slot in reversed(others):
            copy4(slot, index).start()
        yrecv[light, index] = ysend[light, index]
    whole[...] = basis
    rows_ref[...] = whole[own_rows(0, rows), :]
    for finish in finishes:
        finish()
    for slot in others:
        for block in range(blocks):
            first_copy(slot, block).wait_send()
        if parts > 2:
            bulk_copy(slot).wait_send()
        for q in range(pieces if parts > 1 else 0):
            chunk_copy(slot, q).wait_send()
    for index in range(parts):
        for slot in others:
            copy4(slot, index).wait_recv()
        for k in range(lights):
            for q in range(pieces):
                core_ref[:, k * parts + index, q * piece : (q + 1) * piece] = yrecv[k, index, q].astype(
                    core_ref.dtype
                )
    for index in range(parts):
        for slot in others:
            copy4(slot, index).wait_send()


def settle_kernel(core_ref, rows_ref, core_out, rows_out, sems):
    copies = [
        pltpu.make_async_copy(core_ref, core_out, sems.at[0]),
        pltpu.make_async_copy(rows_ref, rows_out, sems.at[1]),
    ]
    for copy in copies:
        copy.start()
    for copy in copies:
        copy.wait()


def settle(core, rows):
    vmem, hbm = pl.BlockSpec(memory_space=pltpu.VMEM), pl.BlockSpec(memory_space=pltpu.HBM)
    return pl.pallas_call(
        settle_kernel,
        out_shape=(jax.ShapeDtypeStruct(core.shape, core.dtype), jax.ShapeDtypeStruct(rows.shape, rows.dtype)),
        in_specs=[vmem, vmem],
        out_specs=(hbm, hbm),
        scratch_shapes=[pltpu.SemaphoreType.DMA((2,))],
        compiler_params=pltpu.CompilerParams(vmem_limit_bytes=8 * 1024 * 1024),
    )(core, rows)


def per_device(reflectance, start_basis):
    rows, own_cams, width = reflectance.shape
    rank = start_basis.shape[1]
    lights, pixes, cams = (lax.axis_size(name) for name in ("light", "pix", "cam"))
    plane = pixes * cams
    all_rows, share, parts = rows * lights, rank // lights, own_cams // lights
    scale = 1.0 / (own_cams * width * cams * pixes)
    piece = min(256, width)
    pieces = width // piece
    blocks = max(1, rows // 64)
    shard = all_rows // plane
    subs = 2
    vmem, hbm = pl.BlockSpec(memory_space=pltpu.VMEM), pl.BlockSpec(memory_space=pltpu.HBM)
    dma = pltpu.SemaphoreType.DMA
    bf16, f32 = jnp.bfloat16, jnp.float32
    sub_shape = (subs, shard // subs, rank)
    core, basis_rows = pl.pallas_call(
        functools.partial(step_kernel, lights, pixes, cams, blocks, subs, scale),
        out_shape=(
            jax.ShapeDtypeStruct((share, own_cams, width), f32),
            jax.ShapeDtypeStruct((rows, rank), f32),
        ),
        in_specs=[hbm, hbm],
        out_specs=(vmem, vmem),
        scratch_shapes=[
            pltpu.VMEM((2, rows // blocks, own_cams, width), bf16),
            pltpu.VMEM((own_cams, pieces, rows, piece), bf16),
            pltpu.VMEM((parts, pieces, all_rows, piece), bf16),
            pltpu.VMEM((2 * rank, all_rows), bf16),
            pltpu.VMEM((all_rows, rank), f32),
            pltpu.VMEM((all_rows, all_rows), f32),
            pltpu.VMEM((all_rows, all_rows), bf16),
            pltpu.VMEM((all_rows, rank), f32),
            pltpu.VMEM((all_rows, 2 * rank), bf16),
            pltpu.VMEM((ITERS, all_rows, rank), bf16),
            pltpu.VMEM((ITERS, plane - 1) + sub_shape, bf16),
            pltpu.VMEM((ITERS,) + sub_shape, bf16),
            pltpu.VMEM((ITERS, lights) + sub_shape, bf16),
            pltpu.VMEM((ITERS, all_rows, rank), bf16),
            pltpu.VMEM((lights, parts, pieces, share, piece), bf16),
            pltpu.VMEM((lights, parts, pieces, share, piece), bf16),
            dma((2,)), dma((parts,)), dma,
            dma((lights - 1, blocks)), dma((lights - 1, blocks)),
            dma((lights - 1,)), dma((lights - 1,)), dma((lights - 1, pieces)), dma((lights - 1, pieces)),
            dma((ITERS, plane - 1, subs)), dma((ITERS, plane - 1, subs)),
            dma((ITERS, lights - 1, subs)), dma((ITERS, lights - 1, subs)),
            dma((ITERS, plane - 1, subs)), dma((ITERS, plane - 1, subs)),
            dma((lights - 1, parts)), dma((lights - 1, parts)),
        ],
        compiler_params=pltpu.CompilerParams(
            collective_id=0, has_side_effects=True, vmem_limit_bytes=44 * 1024 * 1024
        ),
    )(reflectance, pltpu.with_memory_space_constraint(start_basis, pltpu.HBM))
    return settle(core, basis_rows)


def solution(mesh):
    return jax.shard_map(
        per_device,
        mesh=mesh,
        in_specs=(P("light", "cam", "pix"), P()),
        out_specs=(P("light", "cam", "pix"), P("light", None)),
        check_vma=False,
    )
```
